128 devices in a mesh: wide: 8 (over y, core), narrow: 16 (over x, z).
Axes of the slice: x: 4, y: 4, z: 4, core: 2. Of those that a mesh axis runs over, the one named last changes fastest.
Arguments:
- samples: bfloat16 [16384, 1024], P(('wide', 'narrow')), may hold values from -6 to 6
- clusters: int32 [16384, 4], P(('wide', 'narrow')), may hold values from 0 to 16383, all different within a row
- blocks: int32 [16384, 8], P(('wide', 'narrow')), may hold values from 0 to 127, all different within a row; in each aligned block of 128 rows (0 to 127, 128 to 255, ...) at most 10 rows name the same one
- labels: int32 [16384, 8], P(('wide', 'narrow')), may hold values from 0 to 2047
- coarse_weight: bfloat16 [1024, 16384], P(None, 'narrow'), may hold values from -0.1875 to 0.1875
- coarse_moment: float32 [1024, 16384], P('wide', 'narrow'), may hold values from -180 to 180
- fine_weight: bfloat16 [128, 1024, 2048], P(('wide', 'narrow')), may hold values from -0.1875 to 0.1875
- fine_moment: float32 [128, 1024, 2048], P(('wide', 'narrow')), may hold values from -60 to 60
Outputs:
- row_grads: float32 [16384, 1024], P(('wide', 'narrow'))
- new_coarse: float32 [1024, 16384], P('wide', 'narrow')
- new_fine: float32 [128, 1024, 2048], P(('wide', 'narrow'))
The draws below stay inside these ranges and needn't reach their ends.
Inputs may be any that keep to these rules, and one draw needn't show every extreme that they name: Each row names 4 different clusters. Each row names 8 different fine blocks; among the rows of one device no block is named more than 10 times, and some block is named exactly 10 times.
All inputs are finite; a program needn't handle non-finite values.
Results may differ from the reference program's by a relative error of at most 0.0023.
Values may be sent and summed in bfloat16 or wider, within the bound.
No kernel may reach another device: no remote copies, remote signals or barrier semaphores. Data moves between devices by JAX's collectives and lax.ppermute only.
A program may use at most 192 MiB of HBM per device.

```python
import math
import jax
import jax.numpy as jnp
import numpy as np
from jax import lax

D = 1024
FB = 2048
TOPC = 4
TOPB = 8
ROW_DEV = 128
ROWS = 16384
CLUSTERS = 16384
BLOCKS = 128
CAP = 10
N_WIDE = 8
N_NARROW = 16


def touch_ends(entries, stream_key, least, largest):
    spot = [jax.random.randint(jax.random.fold_in(stream_key, axis), (), 0, length) for axis, length in enumerate(entries.shape)]
    longest = entries.shape.index(max(entries.shape))
    beside = spot[:longest] + [(spot[longest] + 1) % entries.shape[longest]] + spot[longest + 1:]
    return entries.at[tuple(spot)].set(least).at[tuple(beside)].set(largest)


def levels(rng, dims, shards, smallest, high):
    def one(position, shards_of):
        draws = jax.random.uniform(jax.random.fold_in(jax.random.fold_in(rng, 6), position), (shards_of,), jnp.float32, smallest / len(shards), high / len(shards))
        return jnp.repeat(jnp.exp(draws), dims[position] // shards_of).reshape((-1,) + (1,) * (len(dims) - position - 1))

    gain = one(*shards[0])
    for cut in shards[1:]:
        gain = gain * one(*cut)
    return gain


def picks_of(stream_key, rows, count, top, lift):
    sequence = jax.random.permutation(jax.random.fold_in(stream_key, 1), count)
    favour = sequence
    for power in range(3):
        favour = favour * favour // count
    favour = favour * lift // count
    chance = jax.random.randint(jax.random.fold_in(stream_key, 2), (rows, count), 0, 4096) + favour
    fixed_rows = jax.random.permutation(jax.random.fold_in(stream_key, 3), rows)[jnp.arange(count) % rows]
    chance = jnp.where(jnp.arange(rows)[:, None] == fixed_rows[None, :], 1 << 14, chance)
    score = chance * count + jnp.arange(count)
    return lax.top_k(score.astype(jnp.int32), top)[1].astype(jnp.int32)


def assign_block(stream_key, own, number, rows, count, top, most, skew):
    sequence = jax.random.permutation(stream_key, count)
    crowded, ordinary = load_shares(count, rows * top, most, skew, True), load_shares(count, rows * top, most, skew, False)
    places = jnp.arange(count)

    def named(tallies, rotation):
        used = int((tallies > 0).sum())
        fixed = max(1, used // 4)
        passed = fixed + (places - fixed + rotation * (used - fixed)) % max(1, count - fixed)
        return jnp.zeros((count,), jnp.int32).at[sequence[jnp.where(places < fixed, places, passed)]].set(jnp.asarray(tallies, jnp.int32))

    tallies = jnp.where(number % 4 == 0, named(crowded, number // 4), named(ordinary, number - number // 4 - 1))
    mixed = jax.random.permutation(jax.random.fold_in(own, 3), count)
    source_of, taker = mixed[0:count // 2 * 2:2], mixed[1:count // 2 * 2:2]
    slack = jnp.minimum(tallies[source_of] - 1, most - tallies[taker]) // 2
    slack = jnp.where((source_of == sequence[0]) | (taker == sequence[0]) | (tallies[taker] == 0), 0, jnp.maximum(slack, 0))
    passed = jax.random.randint(jax.random.fold_in(own, 4), (count // 2,), 0, 1 << 20) % (slack + 1)
    tallies = tallies.at[source_of].add(-passed).at[taker].add(passed)
    members = jnp.searchsorted(jnp.cumsum(tallies), jnp.arange(rows * top), side="right").astype(jnp.int32)
    grid = members.reshape(top, rows).T
    grid = grid[jax.random.permutation(jax.random.fold_in(own, 1), rows)]
    rotation = jax.random.randint(jax.random.fold_in(own, 2), (rows, 1), 0, top)
    return jnp.take_along_axis(grid, (jnp.arange(top)[None, :] + rotation) % top, axis=1)


def load_shares(number_of, total, bound, skew, full):
    loads = [(1 << 20) // math.isqrt(grade ** skew) + 1 for grade in range(1, number_of + 1)]
    largest = bound if full else min(bound, max(-(-total // number_of), total * loads[0] // sum(loads)))
    least = 1 if total - largest >= number_of - 1 else 0
    holding, rest = [largest] + [least] * (number_of - 1), total - largest - least * (number_of - 1)
    while rest > 0:
        candidates = [i for i in range(1, number_of) if holding[i] < largest] or [i for i in range(1, number_of) if holding[i] < bound]
        pool, left = sum([loads[i] for i in candidates]), rest
        for i in candidates:
            addition = min(bound - holding[i], max(1, left * loads[i] // pool), rest)
            holding[i] = holding[i] + addition
            rest = rest - addition
    return np.array(holding)


def noise(key, dims, scale, limit, shards=(), kind=jnp.bfloat16):
    loudness = levels(key, dims, shards, -0.22, 0.18) if shards else 1.0
    array = jax.random.normal(key, dims, jnp.float32) * scale * loudness
    return jnp.minimum(jnp.maximum(array, -limit), limit).astype(kind)


def setup_inputs(seed: int = 0) -> dict:
    keys = jax.random.split(jax.random.key(seed), 9)
    samples = noise(keys[0], (ROWS, D), 1.0, 6.0, ((0, 128),))
    clusters = picks_of(keys[1], ROWS, CLUSTERS, TOPC, 2)
    blocks_keys = jax.random.split(jax.random.fold_in(keys[2], 1), ROWS // ROW_DEV)
    blocks_turns = jax.random.permutation(jax.random.fold_in(keys[2], 3), ROWS // ROW_DEV)
    blocks = jax.vmap(lambda own, number: assign_block(jax.random.fold_in(keys[2], 2), own, number, ROW_DEV, BLOCKS, TOPB, CAP, 2))(blocks_keys, blocks_turns).reshape((ROWS, TOPB))
    labels = touch_ends(jax.random.randint(keys[3], (ROWS, TOPB), 0, FB), jax.random.fold_in(keys[3], 1), 0, FB - 1).astype(jnp.int32)
    coarse_weight = noise(keys[4], (D, CLUSTERS), D ** -0.5, 0.1875, ((1, 16),))
    coarse_moment = noise(keys[5], (D, CLUSTERS), 30.0, 180.0, ((0, 8), (1, 16)), jnp.float32)
    fine_weight = noise(keys[6], (BLOCKS, D, FB), D ** -0.5, 0.1875, ((0, 128),))
    fine_moment = noise(keys[7], (BLOCKS, D, FB), 10.0, 60.0, ((0, 128),), jnp.float32)
    return dict(samples=samples, clusters=clusters, blocks=blocks, labels=labels, coarse_weight=coarse_weight, coarse_moment=coarse_moment, fine_weight=fine_weight, fine_moment=fine_moment)


BETA = 0.9


def reference(samples, clusters, blocks, labels, coarse_weight, coarse_moment, fine_weight, fine_moment):
    column_ids = jnp.arange(CLUSTERS, dtype=jnp.int32)
    group_rows = ROW_DEV * N_NARROW

    def coarse_step(running, inputs):
        row_block, clu_block = inputs
        scores = jnp.dot(row_block, coarse_weight, preferred_element_type=jnp.float32)
        target = jnp.any(clu_block[:, :, None] == column_ids[None, None, :], axis=1)
        grad_block = (jax.nn.sigmoid(scores) - target.astype(jnp.float32)).astype(jnp.bfloat16)
        running = running + lax.dot_general(row_block, grad_block, (((0,), (0,)), ((), ())), preferred_element_type=jnp.float32)
        row_part = lax.dot_general(grad_block, coarse_weight, (((1,), (1,)), ((), ())), preferred_element_type=jnp.float32)
        return running, row_part

    start_sum = jnp.zeros((D, CLUSTERS), jnp.float32)
    weight_grad, coarse_rows = lax.scan(coarse_step, start_sum, (samples.reshape(N_WIDE, group_rows, D), clusters.reshape(N_WIDE, group_rows, TOPC)))
    new_coarse = BETA * coarse_moment + weight_grad

    pair_count = ROWS * TOPB
    slot_total = N_WIDE * N_NARROW * CAP
    pair_blocks = blocks.reshape(-1)
    pair_labels = labels.reshape(-1)
    label_ids = jnp.arange(FB, dtype=jnp.int32)

    def fine_step(running, inputs):
        weight, moment, block_id = inputs
        pair_index = jnp.nonzero(pair_blocks == block_id, size=slot_total, fill_value=pair_count)[0].astype(jnp.int32)
        filled = pair_index < pair_count
        safe_index = jnp.where(filled, pair_index, 0)
        row_index = safe_index // TOPB
        slot_rows = jnp.where(filled[:, None], samples[row_index], jnp.zeros((), samples.dtype))
        scores = jnp.dot(slot_rows, weight, preferred_element_type=jnp.float32)
        onehot = (pair_labels[safe_index][:, None] == label_ids[None, :]).astype(jnp.float32)
        grad_slots = jnp.where(filled[:, None], jax.nn.sigmoid(scores) - onehot, 0.0).astype(jnp.bfloat16)
        weight_part = lax.dot_general(slot_rows, grad_slots, (((0,), (0,)), ((), ())), preferred_element_type=jnp.float32)
        slot_grads = lax.dot_general(grad_slots, weight, (((1,), (1,)), ((), ())), preferred_element_type=jnp.float32)
        running = running.at[row_index].add(jnp.where(filled[:, None], slot_grads, 0.0))
        return running, BETA * moment + weight_part

    fine_rows, new_fine = lax.scan(fine_step, jnp.zeros((ROWS, D), jnp.float32), (fine_weight, fine_moment, jnp.arange(BLOCKS, dtype=jnp.int32)))
    return coarse_rows.reshape(ROWS, D) + fine_rows, new_coarse, new_fine
```

```python
import jax
import jax.numpy as jnp
from jax import lax
from jax.sharding import PartitionSpec as P

BETA = 0.9
AXES = ("wide", "narrow")
SIDE = 4


def device_map(move):
    pairs = []
    for y in range(SIDE):
        for core in range(2):
            for x in range(SIDE):
                for z in range(SIDE):
                    tx, ty, tz, tc = move(x, y, z, core)
                    target = ((ty % SIDE) * 2 + tc) * 16 + (tx % SIDE) * 4 + tz % SIDE
                    pairs.append(((y * 2 + core) * 16 + x * 4 + z, target))
    return pairs


def first_line(step):
    return device_map(lambda x, y, z, c: (x, y, z + step, c) if c == 0 else (x + step, y, z, c))


def second_line(step):
    return device_map(lambda x, y, z, c: (x + step, y, z, c) if c == 0 else (x, y, z + step, c))


def send(value, pairs):
    return lax.ppermute(value, AXES, pairs)


STEPS = (0, 1, -1, 2)


def on_device(
    samples, clusters, blocks, labels, coarse_weight, coarse_moment, fine_weight, fine_moment
):
    f32, bf16 = jnp.float32, jnp.bfloat16
    rows_here, width = samples.shape
    wide_count = lax.axis_size("wide")
    narrow_count = lax.axis_size("narrow")
    picked = blocks.shape[1]
    owners = wide_count * narrow_count
    capacity = 5 * rows_here * picked // (4 * owners)
    group = SIDE * capacity
    columns = coarse_weight.shape[1]
    narrow_at = lax.axis_index("narrow")

    top = clusters.shape[1]
    notes = jnp.concatenate([blocks.T, labels.T, clusters.T], axis=0)
    note_line = [notes] + [send(notes, first_line(s)) for s in STEPS[1:]]
    line = [samples] + [send(samples, first_line(s)) for s in STEPS[1:]]
    note_line = jnp.stack(note_line)
    note_chunks = [note_line] + [send(note_line, second_line(s)) for s in STEPS[1:]]
    line = jnp.concatenate(line, axis=0)
    chunks = [line] + [send(line, second_line(s)) for s in STEPS[1:]]

    notes_all = jnp.stack(note_chunks)
    block_all = notes_all[:, :, :picked]
    label_all = notes_all[:, :, picked : 2 * picked]
    mine = jnp.arange(wide_count, dtype=jnp.int32) * narrow_count + narrow_at
    same = block_all[:, None] == mine[None, :, None, None, None]
    hit = jnp.any(same, axis=3)
    hit_label = jnp.sum(jnp.where(same, label_all[:, None] + 1, 0), axis=3)
    before = (
        jnp.arange(rows_here)[:, None] < jnp.arange(rows_here)[None, :]
    ).astype(bf16)
    position = jnp.dot(hit.astype(bf16), before, preferred_element_type=f32).astype(jnp.int32)
    slot = jnp.where(
        hit, position + capacity * jnp.arange(SIDE, dtype=jnp.int32)[None, None, :, None], -1
    ).reshape(SIDE, wide_count, 1, SIDE * rows_here)
    hit_label = hit_label.reshape(SIDE, wide_count, 1, SIDE * rows_here)
    chosen = slot == jnp.arange(group, dtype=jnp.int32)[None, None, :, None]
    slot_label = jnp.sum(jnp.where(chosen, hit_label, 0), axis=3) - 1
    chosen = chosen.astype(bf16).reshape(SIDE, wide_count * group, SIDE * rows_here)
    owner_labels = lax.all_to_all(
        jnp.swapaxes(slot_label, 0, 1), "wide", split_axis=0, concat_axis=0, tiled=True
    )
    owner_labels = jnp.swapaxes(owner_labels, 0, 1).reshape(SIDE, wide_count * group)

    weight = fine_weight[0]
    label_ids = jnp.arange(weight.shape[1], dtype=jnp.int32)
    column_ids = narrow_at * columns + jnp.arange(columns, dtype=jnp.int32)

    arrived = []
    for k in range(SIDE):
        outgoing = jnp.dot(chosen[k], chunks[k], preferred_element_type=f32).astype(bf16)
        outgoing = outgoing.reshape(wide_count, group, width)
        got = lax.all_to_all(outgoing, "wide", split_axis=0, concat_axis=0, tiled=True)
        arrived.append(got.reshape(wide_count * group, width))

    coarse_grads, coarse_rows = [], []
    for k in range(SIDE):
        logits = jnp.dot(chunks[k], coarse_weight, preferred_element_type=f32)
        named = notes_all[k, :, 2 * picked :]
        named = jnp.swapaxes(named, 1, 2).reshape(SIDE * rows_here, top)
        target = named[:, 0:1] == column_ids[None, :]
        for t in range(1, top):
            target = target | (named[:, t : t + 1] == column_ids[None, :])
        grad = (jax.nn.sigmoid(logits) - target.astype(f32)).astype(bf16)
        coarse_grads.append(grad)
        coarse_rows.append(
            lax.dot_general(
                grad, coarse_weight, (((1,), (1,)), ((), ())), preferred_element_type=f32
            )
        )

    fine_grads, returned = [], []
    for k in range(SIDE):
        fine_logits = jnp.dot(arrived[k], weight, preferred_element_type=f32)
        onehot = (owner_labels[k][:, None] == label_ids[None, :]).astype(f32)
        grad = jnp.where(
            (owner_labels[k] >= 0)[:, None], jax.nn.sigmoid(fine_logits) - onehot, 0.0
        ).astype(bf16)
        fine_grads.append(grad)
        slot_grads = lax.dot_general(
            grad, weight, (((1,), (1,)), ((), ())), preferred_element_type=f32
        ).astype(bf16)
        back = lax.all_to_all(
            slot_grads.reshape(wide_count, group, width),
            "wide",
            split_axis=0,
            concat_axis=0,
            tiled=True,
        )
        returned.append(back.reshape(wide_count * group, width))

    weight_part = lax.dot_general(
        jnp.concatenate(chunks, axis=0),
        jnp.concatenate(coarse_grads, axis=0),
        (((0,), (0,)), ((), ())),
        preferred_element_type=f32,
    ).astype(bf16)
    weight_parts = lax.all_to_all(
        weight_part.reshape(wide_count, width // wide_count, columns),
        "wide",
        split_axis=0,
        concat_axis=0,
        tiled=True,
    )
    new_coarse = BETA * coarse_moment + jnp.sum(weight_parts.astype(f32), axis=0)

    fine_share = lax.dot_general(
        jnp.concatenate(arrived, axis=0),
        jnp.concatenate(fine_grads, axis=0),
        (((0,), (0,)), ((), ())),
        preferred_element_type=f32,
    )
    new_fine = BETA * fine_moment + fine_share[None]

    partial = [
        coarse_rows[k]
        + lax.dot_general(
            chosen[k], returned[k], (((0,), (0,)), ((), ())), preferred_element_type=f32
        )
        for k in range(SIDE)
    ]
    total = partial[0]
    for k in (3, 1, 2):
        total = total + send(partial[k].astype(bf16), second_line(-STEPS[k])).astype(f32)
    total = total.reshape(SIDE, rows_here, width)
    result = total[0]
    for j in (3, 1, 2):
        result = result + send(total[j], first_line(-STEPS[j]))
    return (result, new_coarse, new_fine)


def solution(mesh):
    in_specs = (
        P(("wide", "narrow"), None),
        P(("wide", "narrow"), None),
        P(("wide", "narrow"), None),
        P(("wide", "narrow"), None),
        P(None, "narrow"),
        P("wide", "narrow"),
        P(("wide", "narrow"), None, None),
        P(("wide", "narrow"), None, None),
    )
    out_specs = (
        P(("wide", "narrow"), None),
        P("wide", "narrow"),
        P(("wide", "narrow"), None, None),
    )
    return jax.shard_map(
        on_device, mesh=mesh, in_specs=in_specs, out_specs=out_specs, check_vma=False
    )
```

```python
import functools

import jax
import jax.numpy as jnp
from jax import lax
from jax.experimental import pallas as pl
from jax.experimental.pallas import tpu as pltpu
from jax.sharding import PartitionSpec as P


BETA = 0.9
AXES = ("wide", "narrow")
SIDE = 4
STEPS = (0, 1, -1, 2)
DIGIT = 128
F32, BF16 = jnp.float32, jnp.bfloat16


def device_map(move):
    pairs = []
    for y in range(SIDE):
        for core in range(2):
            for x in range(SIDE):
                for z in range(SIDE):
                    tx, ty, tz, tc = move(x, y, z, core)
                    target = ((ty % SIDE) * 2 + tc) * 16 + (tx % SIDE) * 4 + tz % SIDE
                    pairs.append(((y * 2 + core) * 16 + x * 4 + z, target))
    return pairs


def first_line(step):
    return device_map(lambda x, y, z, c: (x, y, z + step, c) if c == 0 else (x + step, y, z, c))


def second_line(step):
    return device_map(lambda x, y, z, c: (x + step, y, z, c) if c == 0 else (x, y, z + step, c))


def column_map(step):
    return device_map(lambda x, y, z, c: (x, y + step, z, c))


def partner_map():
    return device_map(lambda x, y, z, c: (x, y, z, 1 - c))


def send(value, pairs):
    return lax.ppermute(value, AXES, pairs)


def after(value, *earlier):
    return lax.optimization_barrier((value, *earlier))[0]


def swap_wide(value):
    return lax.all_to_all(value, "wide", split_axis=0, concat_axis=0, tiled=True)


def sigmoid(x):
    return 0.5 * jnp.tanh(0.5 * x) + 0.5


def dot(a, b, left, right):
    return lax.dot_general(a, b, (((left,), (right,)), ((), ())), preferred_element_type=F32)


def stored(shape):
    if isinstance(shape, tuple):
        return tuple(stored(one) for one in shape)
    return pltpu.HBM(shape.shape, shape.dtype)


def call(body, grid, in_specs, out_specs, out_shape, flops, scratch=(), aliases=None):
    return pl.pallas_call(
        body,
        grid=grid,
        in_specs=in_specs,
        out_specs=out_specs,
        out_shape=stored(out_shape),
        scratch_shapes=scratch,
        input_output_aliases=aliases or {},
        compiler_params=pltpu.CompilerParams(vmem_limit_bytes=48 << 20),
        cost_estimate=pl.CostEstimate(flops=flops, transcendentals=0, bytes_accessed=flops // 1000),
    )


def whole(array):
    return pl.BlockSpec(array.shape, lambda i: (0,) * array.ndim)


def selection(slots, size):
    count, rows = slots.shape
    table = jnp.concatenate(
        [jnp.broadcast_to(slots[q : q + 1], (size, rows)) for q in range(count)], axis=0
    )
    place = lax.broadcasted_iota(jnp.int32, (size, 1), 0)
    place = jnp.concatenate([place] * count, axis=0)
    return (table == place).astype(F32).astype(BF16)


def compact_body(row_ref, slot_ref, *refs):
    out_ref = refs[-1]
    count, size = out_ref.shape[:2]
    picked = dot(selection(slot_ref[...], size), row_ref[...], 1, 0)
    for q in range(count):
        out_ref[q] = picked[q * size : (q + 1) * size].astype(BF16)


def compact(rows, slots, message, place, size, total):
    count, width = slots.shape[0], rows.shape[1]
    earlier = () if message is None else (message,)
    return call(
        compact_body,
        (1,),
        [whole(rows), whole(slots)] + [pl.BlockSpec(memory_space=pl.ANY) for _ in earlier],
        pl.BlockSpec((count, size, width), lambda i: (0, place, 0)),
        jax.ShapeDtypeStruct((count, total, width), BF16),
        2 * count * size * width * rows.shape[0],
        aliases={2: 0} if earlier else None,
    )(rows, slots, *earlier)


def prepare_body(picked, capacity, mine_ref, *refs):
    notes, (slot_ref, spare_ref) = refs[:-2], refs[-2:]
    sources, _, rows = notes[0].shape
    count = mine_ref.shape[0]
    mine = mine_ref[...]
    hits, tags = [], []
    for note in notes:
        for j in range(sources):
            hit = jnp.zeros((count, rows), F32)
            tag = jnp.zeros((count, rows), F32)
            for k in range(picked):
                same = note[j, k : k + 1, :] == mine
                label = note[j, picked + k : picked + k + 1, :].astype(F32) + 1.0
                hit = jnp.where(same, 1.0, hit)
                tag = jnp.where(same, jnp.broadcast_to(label, tag.shape), tag)
            hits.append(hit)
            tags.append(tag)
    one = lax.broadcasted_iota(jnp.int32, (rows, rows), 0)
    two = lax.broadcasted_iota(jnp.int32, (rows, rows), 1)
    before = (one < two).astype(F32).astype(BF16)
    places = dot(jnp.concatenate(hits, axis=0).astype(BF16), before, 1, 0)
    spare_ref[...] = jnp.zeros(spare_ref.shape, spare_ref.dtype)
    size = sources * capacity
    for k in range(len(notes)):
        for j in range(sources):
            at = k * sources + j
            place = places[at * count : (at + 1) * count] + float(j * capacity)
            slot = jnp.where(hits[at] > 0.0, place, -1.0)
            slot_ref[k, :, j * rows : (j + 1) * rows] = slot.astype(jnp.int32)
        tag = jnp.concatenate(tags[k * sources : (k + 1) * sources], axis=1)
        high = jnp.floor(tag * (1.0 / DIGIT))
        digits = jnp.concatenate([high, tag - high * DIGIT], axis=0).astype(BF16)
        found = dot(digits, selection(slot_ref[k], size), 1, 1)
        owner = lax.broadcasted_iota(jnp.int32, found.shape, 0)
        owner = jnp.where(owner >= count, owner - count, owner)
        lane = lax.broadcasted_iota(jnp.int32, found.shape, 1) - owner * size
        found = jnp.where((lane >= 0) & (lane < size), found, 0.0)
        spare_ref[k : k + 1, : count * size] = jnp.sum(found[:count], axis=0, keepdims=True)
        low = jnp.sum(found[count:], axis=0, keepdims=True)
        spare_ref[len(notes) + k : len(notes) + k + 1, : count * size] = low


def prepare(mine, notes, picked, capacity, width):
    sources, _, rows = notes[0].shape
    out = (
        jax.ShapeDtypeStruct((len(notes), mine.shape[0], sources * rows), jnp.int32),
        jax.ShapeDtypeStruct((2 * len(notes), width), F32),
    )
    inputs = [mine, *notes]
    return call(
        functools.partial(prepare_body, picked, capacity),
        (1,),
        [whole(a) for a in inputs],
        tuple(whole(a) for a in out),
        out,
        1 << 28,
    )(*inputs)


def stamp_body(spare_ref, out_ref):
    for q in range(out_ref.shape[0]):
        out_ref[q] = spare_ref[...].astype(BF16)


def stamp(spare, count, size):
    lines, width = spare.shape
    last = size // lines
    return call(
        stamp_body,
        (1,),
        [whole(spare)],
        pl.BlockSpec((count, lines, width), lambda i: (0, last, 0)),
        jax.ShapeDtypeStruct((count, size + lines, width), BF16),
        1 << 20,
    )(spare)


def coarse_body(
    steps, top, row_ref, weight_ref, note_ref, id_ref, grad_ref, part_ref, total_ref, name_ref
):
    step = pl.program_id(0)
    rows = note_ref.shape[2]

    @pl.when(step == 0)
    def _():
        for j in range(note_ref.shape[0]):
            name_ref[j * rows : (j + 1) * rows, :] = note_ref[j, -8:, :].astype(F32).T

    weight = weight_ref[...]
    logits = dot(row_ref[...], weight, 1, 0)
    names, ids = name_ref[...], id_ref[...]
    target = names[:, 0:1] == ids
    for t in range(1, top):
        target = target | (names[:, t : t + 1] == ids)
    grad = sigmoid(logits)
    grad = jnp.where(target, grad - 1.0, grad).astype(BF16)
    grad_ref[...] = grad
    part = dot(grad, weight, 1, 1)

    @pl.when(step == 0)
    def _():
        total_ref[...] = part

    @pl.when((step > 0) & (step < steps - 1))
    def _():
        total_ref[...] += part

    @pl.when(step == steps - 1)
    def _():
        part_ref[...] = (total_ref[...] + part).astype(part_ref.dtype)


def coarse(rows, weight, notes, ids, top, dtype, tile=512):
    count, width = rows.shape
    columns = weight.shape[1]
    steps = columns // tile
    return call(
        functools.partial(coarse_body, steps, top),
        (steps,),
        [
            whole(rows),
            pl.BlockSpec((width, tile), lambda i: (0, i)),
            whole(notes),
            pl.BlockSpec((1, tile), lambda i: (0, i)),
        ],
        (
            pl.BlockSpec((count, tile), lambda i: (0, i)),
            pl.BlockSpec((count, width), lambda i: (0, 0)),
        ),
        (
            jax.ShapeDtypeStruct((count, columns), BF16),
            jax.ShapeDtypeStruct((count, width), dtype),
        ),
        4 * count * width * columns,
        [pltpu.VMEM((count, width), F32), pltpu.VMEM((count, 8), F32)],
    )(rows, weight, notes, ids)


def fine_step(row_ref, weight_ref, grad_ref, total_ref, here_ref):
    step = pl.program_id(0)
    weight = weight_ref[0]
    logits = dot(row_ref[...], weight, 1, 0)
    label = here_ref[...].astype(jnp.int32)
    ids = lax.broadcasted_iota(jnp.int32, logits.shape, 1) + step * logits.shape[1]
    grad = sigmoid(logits)
    grad = jnp.where(label == ids, grad - 1.0, grad)
    grad = jnp.where(label >= 0, grad, 0.0).astype(BF16)
    grad_ref[...] = grad
    part = dot(grad, weight, 1, 1)

    @pl.when(step == 0)
    def _():
        total_ref[...] = part

    @pl.when(step > 0)
    def _():
        total_ref[...] += part


def fine_first_body(
    steps, count, group, row_ref, weight_ref, seat_ref, grad_ref, pair_ref, next_ref, total_ref, here_ref
):
    size = row_ref.shape[0] // count
    rest = next_ref.shape[0] // count

    @pl.when(pl.program_id(0) == 0)
    def _():
        span = count * group
        lane = lax.broadcasted_iota(jnp.int32, (group, span), 1)
        lane = lane - lax.broadcasted_iota(jnp.int32, (group, span), 0)
        mark = lane == seat_ref[:, :1] * group
        here_ref[...] = jnp.full(here_ref.shape, -1.0, F32)
        for q in range(count):
            said = row_ref[(q + 1) * size - 8 : (q + 1) * size, :span].astype(F32)
            said = said[:SIDE] * DIGIT + said[SIDE:]
            for k in range(SIDE):
                table = jnp.broadcast_to(said[k : k + 1], (group, span))
                label = jnp.sum(jnp.where(mark, table, 0.0), axis=1, keepdims=True) - 1.0
                if k < 2:
                    at = q * size + k * group
                    here_ref[at : at + group, :] = label
                else:
                    at = q * rest + (k - 2) * group
                    next_ref[at : at + group, :] = label

    fine_step(row_ref, weight_ref, grad_ref, total_ref, here_ref)

    @pl.when(pl.program_id(0) == steps - 1)
    def _():
        pair_ref[...] = total_ref[...].astype(BF16)


def fine_first(rows, weight, seat, wide_count, group, tile=512):
    count, width = rows.shape
    columns = weight.shape[2]
    steps = columns // tile
    after_rows = 2 * wide_count * group
    return call(
        functools.partial(fine_first_body, steps, wide_count, group),
        (steps,),
        [
            whole(rows),
            pl.BlockSpec((1, width, tile), lambda i: (0, 0, i)),
            whole(seat),
        ],
        (
            pl.BlockSpec((count, tile), lambda i: (0, i)),
            pl.BlockSpec((count, width), lambda i: (0, 0)),
            pl.BlockSpec((after_rows, 1), lambda i: (0, 0)),
        ),
        (
            jax.ShapeDtypeStruct((count, columns), BF16),
            jax.ShapeDtypeStruct((count, width), BF16),
            jax.ShapeDtypeStruct((after_rows, 1), F32),
        ),
        4 * count * width * columns,
        [pltpu.VMEM((count, width), F32), pltpu.VMEM((count, 1), F32)],
    )(rows, weight, seat)


def fine_second_body(
    steps, row_ref, weight_ref, label_ref, pair_ref, order_ref, token_ref, grad_ref, line_ref,
    total_ref, tile_ref,
):
    fine_step(row_ref, weight_ref, grad_ref, total_ref, label_ref)
    count, kept = order_ref.shape
    size, former = row_ref.shape[0] // count, pair_ref.shape[0] // count
    width = total_ref.shape[1]

    @pl.when(pl.program_id(0) == steps - 1)
    def _():
        pieces = width // 128
        split = kept // 2
        old = lax.broadcasted_iota(jnp.int32, (former, kept), 0)
        new = lax.broadcasted_iota(jnp.int32, (size, kept), 0)
        for q in range(count):
            order = order_ref[q : q + 1, :]
            pick = (old == jnp.where(order < split, order, -1)).astype(F32).astype(BF16)
            moved = dot(pick, pair_ref[q * former : (q + 1) * former, :], 0, 0)
            pick = (new == order - split).astype(F32).astype(BF16)
            rows = total_ref[q * size : (q + 1) * size, :].astype(BF16)
            moved = moved + dot(pick, rows, 0, 0)
            for j in range(pieces):
                tile_ref[pl.ds(j, kept, pieces), :] = moved[:, j * 128 : (j + 1) * 128]
            span = kept * pieces
            line_ref[q * span : (q + 1) * span, :] = tile_ref[...].astype(BF16)


def fine_second(rows, weight, labels, pairs, order, token, tile=512):
    count, width = rows.shape
    columns = weight.shape[2]
    steps = columns // tile
    kept = order.shape[1]
    lines = order.shape[0] * kept * (width // 128)
    return call(
        functools.partial(fine_second_body, steps),
        (steps,),
        [
            whole(rows),
            pl.BlockSpec((1, width, tile), lambda i: (0, 0, i)),
            whole(labels),
            whole(pairs),
            whole(order),
            whole(token),
        ],
        (
            pl.BlockSpec((count, tile), lambda i: (0, i)),
            pl.BlockSpec((lines, 128), lambda i: (0, 0)),
        ),
        (
            jax.ShapeDtypeStruct((count, columns), BF16),
            jax.ShapeDtypeStruct((lines, 128), BF16),
        ),
        4 * count * width * columns,
        [pltpu.VMEM((count, width), F32), pltpu.VMEM((kept * (width // 128), 128), F32)],
    )(rows, weight, labels, pairs, order, token)


def finish_body(own_ref, one_ref, two_ref, three_ref, slot_ref, back_ref, out_ref, line_ref):
    total = own_ref[0] + one_ref[...] + two_ref[...] + three_ref[...]
    rows, width = out_ref.shape
    pieces = width // 128
    count = back_ref.shape[0] // pieces
    line_ref[...] = back_ref[...].astype(F32)
    ids = lax.broadcasted_iota(jnp.int32, (rows, count), 1)
    slots = slot_ref[...]
    hit = slots[:, 0:1] == ids
    for k in range(1, slots.shape[1]):
        hit = hit | (slots[:, k : k + 1] == ids)
    pick = hit.astype(F32).astype(BF16)
    for j in range(pieces):
        part = line_ref[pl.ds(j, count, pieces), :].astype(BF16)
        span = slice(j * 128, (j + 1) * 128)
        out_ref[:, span] = total[:, span] + dot(pick, part, 1, 0)


def finish(own, tails, slots, back):
    inputs = [own, *tails, slots, back]
    return call(
        finish_body,
        (1,),
        [pl.BlockSpec((1, *own.shape[1:]), lambda i: (0, 0, 0))] + [whole(a) for a in inputs[1:]],
        whole(tails[0]),
        jax.ShapeDtypeStruct(tails[0].shape, F32),
        2 * own.shape[1] * back.size,
        [pltpu.VMEM(back.shape, F32)],
    )(*inputs)


def outer_body(parts, moment, token_ref, *refs):
    lefts, rights = refs[:parts], refs[parts : 2 * parts]
    left_ref, right_ref = refs[-2:]
    out_ref = refs[-3]
    edge = 0
    for left in lefts:
        left_ref[edge : edge + left.shape[0], :] = left[...]
        edge += left.shape[0]

    @pl.when(pl.program_id(0) == 0)
    def _():
        edge = 0
        for right in rights:
            right_ref[edge : edge + right.shape[0], :] = right[...]
            edge += right.shape[0]

    total = dot(left_ref[...], right_ref[...], 0, 0)
    if moment:
        out_ref[0] = BETA * refs[2 * parts][0] + total
    else:
        out_ref[...] = total.astype(out_ref.dtype)


def outer(token, lefts, rights, moment=None, tile=256):
    width, columns = lefts[0].shape[1], rights[0].shape[1]
    depth = sum(a.shape[0] for a in lefts)
    in_specs = [whole(token)]
    in_specs += [pl.BlockSpec((a.shape[0], tile), lambda i: (0, i)) for a in lefts]
    in_specs += [whole(b) for b in rights]
    inputs = [token, *lefts, *rights]
    if moment is None:
        out_spec = pl.BlockSpec((tile, columns), lambda i: (i, 0))
        out = jax.ShapeDtypeStruct((width, columns), BF16)
    else:
        out_spec = pl.BlockSpec((1, tile, columns), lambda i: (0, i, 0))
        in_specs.append(out_spec)
        inputs.append(moment)
        out = jax.ShapeDtypeStruct((1, width, columns), F32)
    return call(
        functools.partial(outer_body, len(lefts), moment is not None),
        (width // tile,),
        in_specs,
        out_spec,
        out,
        2 * width * columns * depth,
        [pltpu.VMEM((depth, tile), BF16), pltpu.VMEM((depth, columns), BF16)],
    )(*inputs)


def ordered_outer_body(parts, half, order_ref, token_ref, *refs):
    del order_ref, token_ref
    lefts, rights = refs[: 2 * parts], refs[2 * parts : 3 * parts]
    give_ref, keep_ref, left_ref, right_ref = refs[3 * parts :]
    step = pl.program_id(0)
    edge = 0
    for k in range(parts):
        rows, wide = lefts[2 * k].shape
        left_ref[edge : edge + rows, :wide] = lefts[2 * k][...]
        left_ref[edge : edge + rows, wide:] = lefts[2 * k + 1][...]
        edge += rows

    @pl.when(step == 0)
    def _():
        edge = 0
        for right in rights:
            right_ref[edge : edge + right.shape[0], :] = right[...]
            edge += right.shape[0]

    total = dot(left_ref[...], right_ref[...], 0, 0)

    @pl.when(step < half)
    def _():
        give_ref[...] = total

    @pl.when(step >= half)
    def _():
        keep_ref[...] = total


def ordered_outer(order, token, lefts, rights):
    width, columns = lefts[0].shape[1], rights[0].shape[1]
    depth = sum(a.shape[0] for a in lefts)
    tile = width // order.shape[0]
    steps = order.shape[0] // 2
    half = steps // 2
    in_specs = [pl.BlockSpec(token.shape, lambda i, o: (0, 0))]
    inputs = [token]
    for a in lefts:
        in_specs.append(pl.BlockSpec((a.shape[0], tile), lambda i, o: (0, o[2 * i])))
        in_specs.append(pl.BlockSpec((a.shape[0], tile), lambda i, o: (0, o[2 * i + 1])))
        inputs += [a, a]
    in_specs += [pl.BlockSpec(b.shape, lambda i, o: (0, 0)) for b in rights]
    out = jax.ShapeDtypeStruct((width // 2, columns), F32)
    return pl.pallas_call(
        functools.partial(ordered_outer_body, len(lefts), half),
        name="ordered_outer",
        grid_spec=pltpu.PrefetchScalarGridSpec(
            num_scalar_prefetch=1,
            grid=(steps,),
            in_specs=in_specs,
            out_specs=(
                pl.BlockSpec((2 * tile, columns), lambda i, o: (jnp.minimum(i, half - 1), 0)),
                pl.BlockSpec((2 * tile, columns), lambda i, o: (jnp.maximum(i - half, 0), 0)),
            ),
            scratch_shapes=[pltpu.VMEM((depth, 2 * tile), BF16), pltpu.VMEM((depth, columns), BF16)],
        ),
        out_shape=stored((out, out)),
        compiler_params=pltpu.CompilerParams(vmem_limit_bytes=48 << 20),
        cost_estimate=pl.CostEstimate(
            flops=2 * depth * width * columns, transcendentals=0, bytes_accessed=1 << 24
        ),
    )(order, *inputs, *rights)


def step(
    samples, clusters, blocks, labels, coarse_weight, coarse_moment, fine_weight, fine_moment
):
    rows_here, width = samples.shape
    wide_count = lax.axis_size("wide")
    narrow_count = lax.axis_size("narrow")
    picked = blocks.shape[1]
    top = clusters.shape[1]
    owners = wide_count * narrow_count
    capacity = 5 * rows_here * picked // (4 * owners)
    columns = coarse_weight.shape[1]
    narrow_at = lax.axis_index("narrow")
    wide_at = lax.axis_index("wide")
    column_ids = narrow_at * columns + jnp.arange(columns, dtype=jnp.int32)
    column_ids = column_ids[None, :].astype(F32)
    per_chunk = SIDE * capacity
    kept = SIDE * per_chunk

    line = [samples] + [send(samples, first_line(s)) for s in STEPS[1:]]
    line = jnp.concatenate(line, axis=0)
    filler = jnp.full((8 - top, rows_here), -1, jnp.int32)
    notes = jnp.concatenate([blocks.T, labels.T, clusters.T, filler], axis=0)
    note_line = jnp.stack([notes] + [send(notes, first_line(s)) for s in STEPS[1:]])
    note_chunks = [note_line] + [send(note_line, second_line(s)) for s in STEPS[1:]]
    near = [send(line, second_line(s)) for s in STEPS[1:3]]
    rows = [line, *near, None]
    before = (jnp.arange(rows_here)[:, None] < jnp.arange(rows_here)[None, :]).astype(BF16)

    places = jnp.arange(kept, dtype=jnp.int32)
    source_x, source_z = places // capacity // SIDE, places // capacity % SIDE
    step_x = (narrow_at // SIDE - source_x) % SIDE
    step_z = (narrow_at % SIDE - source_z) % SIDE
    turn = jnp.array([STEPS.index(s) for s in (0, 1, 2, -1)], dtype=jnp.int32)
    turn_x = sum(jnp.where(step_x == s, turn[s], 0) for s in range(SIDE))
    turn_z = sum(jnp.where(step_z == s, turn[s], 0) for s in range(SIDE))
    order_0 = turn_x * per_chunk + turn_z * capacity + places % capacity
    order_1 = turn_z * per_chunk + turn_x * capacity + places % capacity
    order = jnp.stack([order_0, order_1] * (wide_count // 2))

    grads, parts = [None] * SIDE, [None] * SIDE

    def coarse_of(k, *earlier):
        grads[k], parts[k] = coarse(
            rows[k],
            coarse_weight,
            note_chunks[k],
            after(column_ids, *earlier),
            top,
            F32 if k == 0 else BF16,
        )
        return parts[k]

    def compact_of(k, message, length, *earlier):
        place = after(slots[k], *earlier) if earlier else slots[k]
        return compact(rows[k], place, message, k % 2, per_chunk, length)

    mine = jnp.arange(wide_count, dtype=jnp.int32) * narrow_count + narrow_at
    mine = jnp.broadcast_to(mine[:, None], (wide_count, rows_here))
    done = coarse_of(0)
    rows[3] = send(after(line, done, *near), second_line(STEPS[3]))
    slots, spare = prepare(after(mine, done), note_chunks, picked, capacity, width)
    half = 2 * per_chunk
    message = stamp(spare, wide_count, half)
    message = compact_of(0, message, half + 8)
    message = compact_of(1, message, half + 8)
    got_1 = swap_wide(message)
    coarse_of(1, message)
    coarse_of(2, parts[1])
    message = compact_of(2, None, half, parts[2])
    message = compact_of(3, message, half)
    got_2 = swap_wide(message)
    coarse_of(3, message)
    shares = []
    for k in (1, 2, 3):
        shares.append(send(after(parts[k], message), second_line(-STEPS[k])).astype(F32))

    y_at, core_at = wide_at // 2, wide_at % 2
    order_y = (y_at + jnp.array(STEPS, dtype=jnp.int32)) % SIDE
    blocks_order = jnp.concatenate([order_y * 2 + 1 - core_at, order_y * 2 + core_at])
    give, keep = ordered_outer(blocks_order, after(column_ids, parts[3]), rows, grads)
    given = send(give, partner_map())
    got_1, got_2 = got_1.reshape(-1, width), got_2.reshape(-1, width)
    seat = jnp.full((1, 128), wide_at, jnp.int32)
    grad_1, pair_1, label_2 = fine_first(
        got_1, fine_weight, after(seat, keep), wide_count, per_chunk
    )
    chip_sum = after(keep, pair_1) + given
    chip_sum = chip_sum.reshape(SIDE, width // wide_count, columns)
    pieces = [send(chip_sum[j].astype(BF16), column_map(STEPS[j])) for j in (1, 2, 3)]
    total = after(parts[0], pair_1)
    for share in shares:
        total = total + share
    total = total.reshape(SIDE, rows_here, width)
    tails = [send(total[j], first_line(-STEPS[j])) for j in (1, 2, 3)]
    grad_2, pairs = fine_second(
        got_2, fine_weight, label_2, pair_1, order, after(column_ids, total, chip_sum)
    )
    pairs = pairs.reshape(owners, -1, 128)
    back = lax.all_to_all(pairs, AXES, split_axis=0, concat_axis=0, tiled=True)

    new_coarse = BETA * after(coarse_moment, pairs) + chip_sum[0]
    for piece in pieces:
        new_coarse = new_coarse + piece.astype(F32)
    blocks = after(blocks, pairs)
    every = jnp.arange(owners, dtype=jnp.int32)
    own_hit = jnp.any(blocks.T[None] == every[:, None, None], axis=1)
    own_place = jnp.dot(own_hit.astype(BF16), before, preferred_element_type=F32)
    own_place = own_place.T.astype(jnp.int32)
    own_slots = blocks * capacity + jnp.sum(
        jnp.where(blocks[:, :, None] == every[None, None, :], own_place[:, None, :], 0), axis=2
    )

    new_fine = outer(
        after(column_ids, pairs), [got_1, got_2], [grad_1, grad_2], fine_moment
    )
    result = finish(total, tails, own_slots, back.reshape(-1, 128))
    return (result, new_coarse, new_fine)


def solution(mesh):
    in_specs = (
        P(("wide", "narrow"), None),
        P(("wide", "narrow"), None),
        P(("wide", "narrow"), None),
        P(("wide", "narrow"), None),
        P(None, "narrow"),
        P("wide", "narrow"),
        P(("wide", "narrow"), None, None),
        P(("wide", "narrow"), None, None),
    )
    out_specs = (
        P(("wide", "narrow"), None),
        P("wide", "narrow"),
        P(("wide", "narrow"), None, None),
    )
    return jax.shard_map(step, mesh=mesh, in_specs=in_specs, out_specs=out_specs, check_vma=False)
```

```python
import functools

import jax
import jax.numpy as jnp
from jax import lax
from jax.experimental import pallas as pl
from jax.experimental.pallas import tpu as pltpu
from jax.sharding import PartitionSpec as P


BETA = 0.9
AXES = ("wide", "narrow")
SIDE = 4
STEPS = (0, 1, -1, 2)
DIGIT = 128
F32, BF16 = jnp.float32, jnp.bfloat16


def device_map(move):
    pairs = []
    for y in range(SIDE):
        for core in range(2):
            for x in range(SIDE):
                for z in range(SIDE):
                    tx, ty, tz, tc = move(x, y, z, core)
                    target = ((ty % SIDE) * 2 + tc) * 16 + (tx % SIDE) * 4 + tz % SIDE
                    pairs.append(((y * 2 + core) * 16 + x * 4 + z, target))
    return pairs


def first_line(step):
    return device_map(lambda x, y, z, c: (x, y, z + step, c) if c == 0 else (x + step, y, z, c))


def second_line(step):
    return device_map(lambda x, y, z, c: (x + step, y, z, c) if c == 0 else (x, y, z + step, c))


def column_map(step):
    return device_map(lambda x, y, z, c: (x, y + step, z, c))


def partner_map():
    return device_map(lambda x, y, z, c: (x, y, z, 1 - c))


def send(value, pairs):
    return lax.ppermute(value, AXES, pairs)


def after(value, *earlier):
    return lax.optimization_barrier((value, *earlier))[0]


def swap_wide(value):
    return lax.all_to_all(value, "wide", split_axis=0, concat_axis=0, tiled=True)


def sigmoid(x):
    return 0.5 * jnp.tanh(0.5 * x) + 0.5


def dot(a, b, left, right):
    return lax.dot_general(a, b, (((left,), (right,)), ((), ())), preferred_element_type=F32)


def stored(shape):
    if isinstance(shape, tuple):
        return tuple(stored(one) for one in shape)
    return pltpu.HBM(shape.shape, shape.dtype)


def from_hbm(*arrays):
    return [pltpu.with_memory_space_constraint(a, pltpu.HBM) for a in arrays]


def call(body, grid, in_specs, out_specs, out_shape, flops, scratch=(), aliases=None):
    return pl.pallas_call(
        body,
        grid=grid,
        in_specs=in_specs,
        out_specs=out_specs,
        out_shape=stored(out_shape),
        scratch_shapes=scratch,
        input_output_aliases=aliases or {},
        compiler_params=pltpu.CompilerParams(vmem_limit_bytes=48 << 20),
        cost_estimate=pl.CostEstimate(flops=flops, transcendentals=0, bytes_accessed=flops // 1000),
    )


def whole(array):
    return pl.BlockSpec(array.shape, lambda i: (0,) * array.ndim)


def selection(slots, size):
    count, rows = slots.shape
    table = jnp.concatenate(
        [jnp.broadcast_to(slots[q : q + 1], (size, rows)) for q in range(count)], axis=0
    )
    place = lax.broadcasted_iota(jnp.int32, (size, 1), 0)
    place = jnp.concatenate([place] * count, axis=0)
    return (table == place).astype(F32).astype(BF16)


def compact_body(row_ref, slot_ref, *refs):
    out_ref = refs[-1]
    count, size = out_ref.shape[:2]
    picked = dot(selection(slot_ref[...], size), row_ref[...], 1, 0)
    for q in range(count):
        out_ref[q] = picked[q * size : (q + 1) * size].astype(BF16)


def compact(rows, slots, message, place, size, total):
    count, width = slots.shape[0], rows.shape[1]
    earlier = () if message is None else (message,)
    return call(
        compact_body,
        (1,),
        [whole(rows), whole(slots)] + [pl.BlockSpec(memory_space=pl.ANY) for _ in earlier],
        pl.BlockSpec((count, size, width), lambda i: (0, place, 0)),
        jax.ShapeDtypeStruct((count, total, width), BF16),
        2 * count * size * width * rows.shape[0],
        aliases={2: 0} if earlier else None,
    )(*from_hbm(rows), slots, *earlier)


def prepare_body(picked, capacity, mine_ref, *refs):
    chunks = len(refs) // 2 - 1
    notes, slot_refs, spare_ref, own_ref = refs[:chunks], refs[chunks:-2], refs[-2], refs[-1]
    sources, _, rows = notes[0].shape
    count = mine_ref.shape[0]
    mine = mine_ref[...]
    hits, tags = [], []
    for note in notes:
        for j in range(sources):
            hit = jnp.zeros((count, rows), F32)
            tag = jnp.zeros((count, rows), F32)
            for k in range(picked):
                same = note[j, k : k + 1, :] == mine
                label = note[j, picked + k : picked + k + 1, :].astype(F32) + 1.0
                hit = jnp.where(same, 1.0, hit)
                tag = jnp.where(same, jnp.broadcast_to(label, tag.shape), tag)
            hits.append(hit)
            tags.append(tag)
    one = lax.broadcasted_iota(jnp.int32, (rows, rows), 0)
    two = lax.broadcasted_iota(jnp.int32, (rows, rows), 1)
    before = (one < two).astype(F32).astype(BF16)
    places = dot(jnp.concatenate(hits, axis=0).astype(BF16), before, 1, 0)
    owners = own_ref.shape[1]
    owner = lax.broadcasted_iota(jnp.int32, (owners, rows), 0)
    chose = [notes[0][0, k : k + 1, :] == owner for k in range(picked)]
    hit = jnp.zeros((owners, rows), F32)
    for same in chose:
        hit = jnp.where(same, 1.0, hit)
    seat = dot(hit.astype(BF16), before, 1, 0) + (owner * capacity).astype(F32)
    for k, same in enumerate(chose):
        own_ref[k : k + 1, :] = jnp.sum(jnp.where(same, seat, 0.0), axis=0, keepdims=True)
    spare_ref[...] = jnp.zeros(spare_ref.shape, spare_ref.dtype)
    size = sources * capacity
    for k in range(len(notes)):
        for j in range(sources):
            at = k * sources + j
            place = places[at * count : (at + 1) * count] + float(j * capacity)
            slot = jnp.where(hits[at] > 0.0, place, -1.0)
            slot_refs[k][:, j * rows : (j + 1) * rows] = slot.astype(jnp.int32)
        tag = jnp.concatenate(tags[k * sources : (k + 1) * sources], axis=1)
        high = jnp.floor(tag * (1.0 / DIGIT))
        digits = jnp.concatenate([high, tag - high * DIGIT], axis=0).astype(BF16)
        found = dot(digits, selection(slot_refs[k][...], size), 1, 1)
        owner = lax.broadcasted_iota(jnp.int32, found.shape, 0)
        owner = jnp.where(owner >= count, owner - count, owner)
        lane = lax.broadcasted_iota(jnp.int32, found.shape, 1) - owner * size
        found = jnp.where((lane >= 0) & (lane < size), found, 0.0)
        spare_ref[k : k + 1, : count * size] = jnp.sum(found[:count], axis=0, keepdims=True)
        low = jnp.sum(found[count:], axis=0, keepdims=True)
        spare_ref[len(notes) + k : len(notes) + k + 1, : count * size] = low


def prepare(mine, notes, picked, capacity, width):
    sources, _, rows = notes[0].shape
    one = jax.ShapeDtypeStruct((mine.shape[0], sources * rows), jnp.int32)
    out = (
        *[one] * len(notes),
        jax.ShapeDtypeStruct((2 * len(notes), width), F32),
        jax.ShapeDtypeStruct((picked, rows), F32),
    )
    inputs = [mine, *notes]
    return call(
        functools.partial(prepare_body, picked, capacity),
        (1,),
        [whole(a) for a in inputs],
        tuple(whole(a) for a in out),
        out,
        1 << 28,
    )(*inputs)


def stamp_body(spare_ref, out_ref):
    for q in range(out_ref.shape[0]):
        out_ref[q] = spare_ref[...].astype(BF16)


def stamp(spare, count, size):
    lines, width = spare.shape
    last = size // lines
    return call(
        stamp_body,
        (1,),
        [whole(spare)],
        pl.BlockSpec((count, lines, width), lambda i: (0, last, 0)),
        jax.ShapeDtypeStruct((count, size + lines, width), BF16),
        1 << 20,
    )(spare)


def coarse_body(
    steps, top, row_ref, weight_ref, note_ref, id_ref, grad_ref, part_ref, total_ref, name_ref
):
    step = pl.program_id(0)
    rows = note_ref.shape[2]

    @pl.when(step == 0)
    def _():
        for j in range(note_ref.shape[0]):
            name_ref[j * rows : (j + 1) * rows, :] = note_ref[j, -8:, :].astype(F32).T

    weight = weight_ref[...]
    logits = dot(row_ref[...], weight, 1, 0)
    names, ids = name_ref[...], id_ref[...]
    target = names[:, 0:1] == ids
    for t in range(1, top):
        target = target | (names[:, t : t + 1] == ids)
    grad = sigmoid(logits)
    grad = jnp.where(target, grad - 1.0, grad).astype(BF16)
    grad_ref[...] = grad
    part = dot(grad, weight, 1, 1)
    if steps == 1:
        part_ref[...] = part.astype(part_ref.dtype)
        return

    @pl.when(step == 0)
    def _():
        total_ref[...] = part

    @pl.when((step > 0) & (step < steps - 1))
    def _():
        total_ref[...] += part

    @pl.when(step == steps - 1)
    def _():
        part_ref[...] = (total_ref[...] + part).astype(part_ref.dtype)


def coarse(rows, weight, notes, ids, top, dtype, tile=1024):
    count, width = rows.shape
    columns = weight.shape[1]
    steps = columns // tile
    return call(
        functools.partial(coarse_body, steps, top),
        (steps,),
        [
            whole(rows),
            pl.BlockSpec((width, tile), lambda i: (0, i)),
            whole(notes),
            pl.BlockSpec((1, tile), lambda i: (0, i)),
        ],
        (
            pl.BlockSpec((count, tile), lambda i: (0, i)),
            pl.BlockSpec((count, width), lambda i: (0, 0)),
        ),
        (
            jax.ShapeDtypeStruct((count, columns), BF16),
            jax.ShapeDtypeStruct((count, width), dtype),
        ),
        4 * count * width * columns,
        [pltpu.VMEM((count, width), F32), pltpu.VMEM((count, 8), F32)],
    )(rows, weight, notes, ids)


def fine_step(row_ref, weight_ref, grad_ref, total_ref, here_ref):
    step = pl.program_id(0)
    weight = weight_ref[0]
    logits = dot(row_ref[...], weight, 1, 0)
    label = here_ref[...].astype(jnp.int32)
    ids = lax.broadcasted_iota(jnp.int32, logits.shape, 1) + step * logits.shape[1]
    grad = sigmoid(logits)
    grad = jnp.where(label == ids, grad - 1.0, grad)
    grad = jnp.where(label >= 0, grad, 0.0).astype(BF16)
    grad_ref[...] = grad
    part = dot(grad, weight, 1, 1)

    @pl.when(step == 0)
    def _():
        total_ref[...] = part

    @pl.when(step > 0)
    def _():
        total_ref[...] += part


def fine_first_body(
    steps, count, group, row_ref, weight_ref, seat_ref, grad_ref, pair_ref, next_ref, total_ref, here_ref
):
    size = row_ref.shape[0] // count
    rest = next_ref.shape[0] // count

    @pl.when(pl.program_id(0) == 0)
    def _():
        span = count * group
        lane = lax.broadcasted_iota(jnp.int32, (group, span), 1)
        lane = lane - lax.broadcasted_iota(jnp.int32, (group, span), 0)
        mark = lane == seat_ref[:, :1] * group
        here_ref[...] = jnp.full(here_ref.shape, -1.0, F32)
        for q in range(count):
            said = row_ref[(q + 1) * size - 8 : (q + 1) * size, :span].astype(F32)
            said = said[:SIDE] * DIGIT + said[SIDE:]
            for k in range(SIDE):
                table = jnp.broadcast_to(said[k : k + 1], (group, span))
                label = jnp.sum(jnp.where(mark, table, 0.0), axis=1, keepdims=True) - 1.0
                if k < 2:
                    at = q * size + k * group
                    here_ref[at : at + group, :] = label
                else:
                    at = q * rest + (k - 2) * group
                    next_ref[at : at + group, :] = label

    fine_step(row_ref, weight_ref, grad_ref, total_ref, here_ref)

    @pl.when(pl.program_id(0) == steps - 1)
    def _():
        pair_ref[...] = total_ref[...].astype(BF16)


def fine_first(rows, weight, seat, wide_count, group, tile=1024):
    count, width = rows.shape
    columns = weight.shape[2]
    steps = columns // tile
    after_rows = 2 * wide_count * group
    return call(
        functools.partial(fine_first_body, steps, wide_count, group),
        (steps,),
        [
            whole(rows),
            pl.BlockSpec((1, width, tile), lambda i: (0, 0, i)),
            whole(seat),
        ],
        (
            pl.BlockSpec((count, tile), lambda i: (0, i)),
            pl.BlockSpec((count, width), lambda i: (0, 0)),
            pl.BlockSpec((after_rows, 1), lambda i: (0, 0)),
        ),
        (
            jax.ShapeDtypeStruct((count, columns), BF16),
            jax.ShapeDtypeStruct((count, width), BF16),
            jax.ShapeDtypeStruct((after_rows, 1), F32),
        ),
        4 * count * width * columns,
        [pltpu.VMEM((count, width), F32), pltpu.VMEM((count, 1), F32)],
    )(*from_hbm(rows, weight), seat)


def fine_second_body(
    steps, row_ref, weight_ref, label_ref, pair_ref, order_ref, token_ref, grad_ref, line_ref,
    total_ref, tile_ref,
):
    fine_step(row_ref, weight_ref, grad_ref, total_ref, label_ref)
    count, kept = order_ref.shape
    size, former = row_ref.shape[0] // count, pair_ref.shape[0] // count
    width = total_ref.shape[1]

    @pl.when(pl.program_id(0) == steps - 1)
    def _():
        pieces = width // 128
        split = kept // 2
        old = lax.broadcasted_iota(jnp.int32, (former, kept), 0)
        new = lax.broadcasted_iota(jnp.int32, (size, kept), 0)
        for q in range(count):
            order = order_ref[q : q + 1, :]
            pick = (old == jnp.where(order < split, order, -1)).astype(F32).astype(BF16)
            moved = dot(pick, pair_ref[q * former : (q + 1) * former, :], 0, 0)
            pick = (new == order - split).astype(F32).astype(BF16)
            rows = total_ref[q * size : (q + 1) * size, :].astype(BF16)
            moved = moved + dot(pick, rows, 0, 0)
            for j in range(pieces):
                tile_ref[pl.ds(j, kept, pieces), :] = moved[:, j * 128 : (j + 1) * 128]
            span = kept * pieces
            line_ref[q * span : (q + 1) * span, :] = tile_ref[...].astype(BF16)


def fine_second(rows, weight, labels, pairs, order, token, tile=512):
    count, width = rows.shape
    columns = weight.shape[2]
    steps = columns // tile
    kept = order.shape[1]
    lines = order.shape[0] * kept * (width // 128)
    return call(
        functools.partial(fine_second_body, steps),
        (steps,),
        [
            whole(rows),
            pl.BlockSpec((1, width, tile), lambda i: (0, 0, i)),
            whole(labels),
            whole(pairs),
            whole(order),
            whole(token),
        ],
        (
            pl.BlockSpec((count, tile), lambda i: (0, i)),
            pl.BlockSpec((lines, 128), lambda i: (0, 0)),
        ),
        (
            jax.ShapeDtypeStruct((count, columns), BF16),
            jax.ShapeDtypeStruct((lines, 128), BF16),
        ),
        4 * count * width * columns,
        [pltpu.VMEM((count, width), F32), pltpu.VMEM((kept * (width // 128), 128), F32)],
    )(*from_hbm(rows, weight, labels, pairs), order, token)


def finish_body(own_ref, one_ref, two_ref, three_ref, slot_ref, back_ref, out_ref, line_ref):
    total = own_ref[0]
    for tail in (one_ref, two_ref, three_ref):
        total = total + tail[...].astype(F32)
    rows, width = out_ref.shape
    pieces = width // 128
    count = back_ref.shape[0] // pieces
    line_ref[...] = back_ref[...].astype(F32)
    ids = lax.broadcasted_iota(jnp.int32, (rows, count), 1)
    slots = slot_ref[...].T.astype(jnp.int32)
    hit = slots[:, 0:1] == ids
    for k in range(1, slots.shape[1]):
        hit = hit | (slots[:, k : k + 1] == ids)
    pick = hit.astype(F32).astype(BF16)
    for j in range(pieces):
        part = line_ref[pl.ds(j, count, pieces), :].astype(BF16)
        span = slice(j * 128, (j + 1) * 128)
        out_ref[:, span] = total[:, span] + dot(pick, part, 1, 0)


def finish(own, tails, slots, back):
    inputs = [own, *tails, slots, back]
    return call(
        finish_body,
        (1,),
        [pl.BlockSpec((1, *own.shape[1:]), lambda i: (0, 0, 0))] + [whole(a) for a in inputs[1:]],
        whole(tails[0]),
        jax.ShapeDtypeStruct(tails[0].shape, F32),
        2 * own.shape[1] * back.size,
        [pltpu.VMEM(back.shape, F32)],
    )(*inputs)


def outer_body(parts, moment, token_ref, *refs):
    lefts, rights = refs[:parts], refs[parts : 2 * parts]
    left_ref, right_ref = refs[-2:]
    out_ref = refs[-3]
    edge = 0
    for left in lefts:
        left_ref[edge : edge + left.shape[0], :] = left[...]
        edge += left.shape[0]

    @pl.when(pl.program_id(0) == 0)
    def _():
        edge = 0
        for right in rights:
            right_ref[edge : edge + right.shape[0], :] = right[...]
            edge += right.shape[0]

    total = dot(left_ref[...], right_ref[...], 0, 0)
    if moment:
        out_ref[0] = BETA * refs[2 * parts][0] + total
    else:
        out_ref[...] = total.astype(out_ref.dtype)


def outer(token, lefts, rights, moment=None, tile=256):
    width, columns = lefts[0].shape[1], rights[0].shape[1]
    depth = sum(a.shape[0] for a in lefts)
    in_specs = [whole(token)]
    in_specs += [pl.BlockSpec((a.shape[0], tile), lambda i: (0, i)) for a in lefts]
    in_specs += [whole(b) for b in rights]
    inputs = [token, *lefts, *rights]
    if moment is None:
        out_spec = pl.BlockSpec((tile, columns), lambda i: (i, 0))
        out = jax.ShapeDtypeStruct((width, columns), BF16)
    else:
        out_spec = pl.BlockSpec((1, tile, columns), lambda i: (0, i, 0))
        in_specs.append(out_spec)
        inputs.append(moment)
        out = jax.ShapeDtypeStruct((1, width, columns), F32)
    return call(
        functools.partial(outer_body, len(lefts), moment is not None),
        (width // tile,),
        in_specs,
        out_spec,
        out,
        2 * width * columns * depth,
        [pltpu.VMEM((depth, tile), BF16), pltpu.VMEM((depth, columns), BF16)],
    )(inputs[0], *from_hbm(*inputs[1:]))


def ordered_outer_body(parts, half, order_ref, token_ref, *refs):
    del order_ref, token_ref
    lefts, rights = refs[: 2 * parts], refs[2 * parts : 3 * parts]
    give_ref, keep_ref, left_ref, right_ref = refs[3 * parts :]
    step = pl.program_id(0)
    edge = 0
    for k in range(parts):
        rows, wide = lefts[2 * k].shape
        left_ref[edge : edge + rows, :wide] = lefts[2 * k][...]
        left_ref[edge : edge + rows, wide:] = lefts[2 * k + 1][...]
        edge += rows

    @pl.when(step == 0)
    def _():
        edge = 0
        for right in rights:
            right_ref[edge : edge + right.shape[0], :] = right[...]
            edge += right.shape[0]

    total = dot(left_ref[...], right_ref[...], 0, 0)

    @pl.when(step < half)
    def _():
        give_ref[...] = total

    @pl.when(step >= half)
    def _():
        keep_ref[...] = total


def ordered_outer(order, token, lefts, rights):
    width, columns = lefts[0].shape[1], rights[0].shape[1]
    depth = sum(a.shape[0] for a in lefts)
    tile = width // order.shape[0]
    steps = order.shape[0] // 2
    half = steps // 2
    in_specs = [pl.BlockSpec(token.shape, lambda i, o: (0, 0))]
    inputs = [token]
    for a in lefts:
        in_specs.append(pl.BlockSpec((a.shape[0], tile), lambda i, o: (0, o[2 * i])))
        in_specs.append(pl.BlockSpec((a.shape[0], tile), lambda i, o: (0, o[2 * i + 1])))
        inputs += [a, a]
    in_specs += [pl.BlockSpec(b.shape, lambda i, o: (0, 0)) for b in rights]
    out = jax.ShapeDtypeStruct((width // 2, columns), F32)
    return pl.pallas_call(
        functools.partial(ordered_outer_body, len(lefts), half),
        name="ordered_outer",
        grid_spec=pltpu.PrefetchScalarGridSpec(
            num_scalar_prefetch=1,
            grid=(steps,),
            in_specs=in_specs,
            out_specs=(
                pl.BlockSpec((2 * tile, columns), lambda i, o: (jnp.minimum(i, half - 1), 0)),
                pl.BlockSpec((2 * tile, columns), lambda i, o: (jnp.maximum(i - half, 0), 0)),
            ),
            scratch_shapes=[pltpu.VMEM((depth, 2 * tile), BF16), pltpu.VMEM((depth, columns), BF16)],
        ),
        out_shape=stored((out, out)),
        compiler_params=pltpu.CompilerParams(vmem_limit_bytes=48 << 20),
        cost_estimate=pl.CostEstimate(
            flops=2 * depth * width * columns, transcendentals=0, bytes_accessed=1 << 24
        ),
    )(order, inputs[0], *from_hbm(*inputs[1:], *rights))


def step(
    samples, clusters, blocks, labels, coarse_weight, coarse_moment, fine_weight, fine_moment
):
    rows_here, width = samples.shape
    wide_count = lax.axis_size("wide")
    narrow_count = lax.axis_size("narrow")
    picked = blocks.shape[1]
    top = clusters.shape[1]
    owners = wide_count * narrow_count
    capacity = 5 * rows_here * picked // (4 * owners)
    columns = coarse_weight.shape[1]
    narrow_at = lax.axis_index("narrow")
    wide_at = lax.axis_index("wide")
    column_ids = narrow_at * columns + jnp.arange(columns, dtype=jnp.int32)
    column_ids = column_ids[None, :].astype(F32)
    per_chunk = SIDE * capacity
    kept = SIDE * per_chunk

    line = [samples] + [send(samples, first_line(s)) for s in STEPS[1:]]
    line = jnp.concatenate(line, axis=0)
    filler = jnp.full((8 - top, rows_here), -1, jnp.int32)
    notes = jnp.concatenate([blocks.T, labels.T, clusters.T, filler], axis=0)
    note_line = jnp.stack([notes] + [send(notes, first_line(s)) for s in STEPS[1:]])
    note_chunks = [note_line] + [send(note_line, second_line(s)) for s in STEPS[1:]]
    near = [send(line, second_line(s)) for s in STEPS[1:3]]
    rows = [line, *near, None]

    places = jnp.arange(kept, dtype=jnp.int32)
    source_x, source_z = places // capacity // SIDE, places // capacity % SIDE
    step_x = (narrow_at // SIDE - source_x) % SIDE
    step_z = (narrow_at % SIDE - source_z) % SIDE
    turn = jnp.array([STEPS.index(s) for s in (0, 1, 2, -1)], dtype=jnp.int32)
    turn_x = sum(jnp.where(step_x == s, turn[s], 0) for s in range(SIDE))
    turn_z = sum(jnp.where(step_z == s, turn[s], 0) for s in range(SIDE))
    order_0 = turn_x * per_chunk + turn_z * capacity + places % capacity
    order_1 = turn_z * per_chunk + turn_x * capacity + places % capacity
    order = jnp.stack([order_0, order_1] * (wide_count // 2))

    grads, parts = [None] * SIDE, [None] * SIDE

    def coarse_of(k, *earlier):
        grads[k], parts[k] = coarse(
            rows[k],
            coarse_weight,
            note_chunks[k],
            after(column_ids, *earlier),
            top,
            F32 if k == 0 else BF16,
        )
        return parts[k]

    def compact_of(k, message, length, *earlier):
        place = after(slots[k], *earlier) if earlier else slots[k]
        return compact(rows[k], place, message, k % 2, per_chunk, length)

    mine = jnp.arange(wide_count, dtype=jnp.int32) * narrow_count + narrow_at
    mine = jnp.broadcast_to(mine[:, None], (wide_count, rows_here))
    done = coarse_of(0)
    *slots, spare, own_slots = prepare(after(mine, done), note_chunks, picked, capacity, width)
    half = 2 * per_chunk
    message = stamp(spare, wide_count, half)
    message = compact_of(0, message, half + 8)
    rows[3] = send(after(line, message, *near), second_line(STEPS[3]))
    message = compact_of(1, message, half + 8)
    got_1 = swap_wide(message)
    coarse_of(1, message)
    coarse_of(2, parts[1])
    message = compact_of(2, None, half, parts[2])
    message = compact_of(3, message, half)
    coarse_of(3, message)
    got_2 = swap_wide(after(message, parts[3]))
    shares = []
    for k in (1, 2, 3):
        shares.append(send(after(parts[k], message), second_line(-STEPS[k])).astype(F32))

    got_1, got_2 = got_1.reshape(-1, width), got_2.reshape(-1, width)
    seat = jnp.full((1, 128), wide_at, jnp.int32)
    grad_1, pair_1, label_2 = fine_first(
        got_1, fine_weight, after(seat, parts[3]), wide_count, per_chunk
    )
    grad_2, pairs = fine_second(
        got_2, fine_weight, label_2, pair_1, order, after(column_ids, pair_1)
    )
    pairs = pairs.reshape(owners, -1, 128)
    back = lax.all_to_all(pairs, AXES, split_axis=0, concat_axis=0, tiled=True)

    y_at, core_at = wide_at // 2, wide_at % 2
    order_y = (y_at + jnp.array(STEPS, dtype=jnp.int32)) % SIDE
    blocks_order = jnp.concatenate([order_y * 2 + 1 - core_at, order_y * 2 + core_at])
    give, keep = ordered_outer(blocks_order, after(column_ids, pairs), rows, grads)
    given = send(give, partner_map())
    total = after(parts[0], keep)
    for share in shares:
        total = total + share
    total = total.reshape(SIDE, rows_here, width)
    tails = [send(total[j].astype(BF16), first_line(-STEPS[j])) for j in (1, 2, 3)]
    chip_sum = after(keep, total) + given
    chip_sum = chip_sum.reshape(SIDE, width // wide_count, columns)
    pieces = [send(chip_sum[j].astype(BF16), column_map(STEPS[j])) for j in (1, 2, 3)]
    new_coarse = BETA * coarse_moment + chip_sum[0]
    for piece in pieces:
        new_coarse = new_coarse + piece.astype(F32)
    new_fine = outer(
        after(column_ids, chip_sum), [got_1, got_2], [grad_1, grad_2], fine_moment
    )
    result = finish(total, tails, own_slots, back.reshape(-1, 128))
    return (result, new_coarse, new_fine)


def solution(mesh):
    in_specs = (
        P(("wide", "narrow"), None),
        P(("wide", "narrow"), None),
        P(("wide", "narrow"), None),
        P(("wide", "narrow"), None),
        P(None, "narrow"),
        P("wide", "narrow"),
        P(("wide", "narrow"), None, None),
        P(("wide", "narrow"), None, None),
    )
    out_specs = (
        P(("wide", "narrow"), None),
        P("wide", "narrow"),
        P(("wide", "narrow"), None, None),
    )
    return jax.shard_map(step, mesh=mesh, in_specs=in_specs, out_specs=out_specs, check_vma=False)
```
